32 devices in a mesh: gx: 4 (over y, x), gy: 2 (over core), zt: 4 (over z).
Axes of the slice: x: 2, y: 2, z: 4, core: 2. Of those that a mesh axis runs over, the one named last changes fastest.
Arguments:
- links: float32 [4, 4, 8, 8, 4, 128], P(None, None, 'zt', 'gx', 'gy'), may hold values from -1 to 1, as said below
- trials: float32 [8, 4, 8, 8, 4, 128], P(None, None, 'zt', 'gx', 'gy'), may hold values from 0.02 to 0.98
- cos_polar: float32 [4, 8, 8, 4, 128], P(None, 'zt', 'gx', 'gy'), may hold values from -0.98 to 0.98
- azimuth: float32 [4, 8, 8, 4, 128], P(None, 'zt', 'gx', 'gy'), may hold values from -3.140625 to 3.140625
- accepted: int32 [4, 8, 8, 4, 128], P(None, 'zt', 'gx', 'gy'), may hold values from 0 to 7
Outputs:
- new_links: float32 [4, 4, 8, 8, 4, 128], P(None, None, 'zt', 'gx', 'gy')
- transporters: float32 [4, 8, 8, 4, 128], P(None, 'zt', 'gx', 'gy')
The draws below stay inside these ranges and needn't reach their ends.
Inputs may be any that keep to these rules, and one draw needn't show every extreme that they name: `links`: every link is a unit quaternion: its four components' squares sum to one.
All inputs are finite; a program needn't handle non-finite values.
Results may differ from the reference program's by a relative error of at most 0.0003.
Values sent between devices are 32-bit elements; how exact they have to be, the bound alone decides.
A program may use at most 64 MiB of HBM per device.

```python
from functools import reduce
import jax
import jax.numpy as jnp
from jax import lax

NZ = 128
NTRIAL = 8
NT = 8
NX = 8
NY = 4


def draw_links(key, part):
    raw = jax.random.normal(key, (4, 4, NT, NX, NY, NZ), jnp.float32)
    return raw / jnp.sqrt(jnp.sum(raw * raw, axis=1, keepdims=True))


def touch_ends(values, stream_key, smallest, high):
    longest = values.shape.index(max(values.shape))
    spots = []
    for shift in (0, 1):
        where = [jax.random.randint(jax.random.fold_in(stream_key, axis), (), 0, length) for axis, length in enumerate(values.shape)]
        where[longest] = (where[longest] + shift) % values.shape[longest]
        spots.append(tuple(where))
    return values.at[spots[0]].set(smallest).at[spots[1]].set(high)


def shard_levels(rng, extent, pieces, least, largest):
    loudness = 1.0
    for axis_at, shards_of in pieces:
        draws = jax.random.uniform(jax.random.fold_in(jax.random.fold_in(rng, 6), axis_at), (shards_of,), jnp.float32, least / len(pieces), largest / len(pieces))
        loudness = loudness * jnp.repeat(jnp.exp(draws), extent[axis_at] // shards_of).reshape((-1,) + (1,) * (len(extent) - 1 - axis_at))
    return loudness


def setup_inputs(seed: int = 0) -> dict:
    seeds = jax.random.split(jax.random.key(seed), 6)
    links = draw_links(jax.random.fold_in(seeds[5], 71), 0)
    trials = jnp.clip(0.02 + 0.96000002 * jax.random.uniform(seeds[1], (NTRIAL, 4, NT, NX, NY, NZ), jnp.float32) ** shard_levels(seeds[1], (NTRIAL, 4, NT, NX, NY, NZ), ((2, 4), (3, 4), (4, 2)), -0.2, 0.2), 0.02, 0.98)
    cos_polar = jnp.clip(jax.random.uniform(seeds[2], (4, NT, NX, NY, NZ), jnp.float32, -0.98, 0.98) * shard_levels(seeds[2], (4, NT, NX, NY, NZ), ((1, 4), (2, 4), (3, 2)), -0.4, 0.0), -0.98, 0.98)
    azimuth = jnp.clip(jax.random.uniform(seeds[3], (4, NT, NX, NY, NZ), jnp.float32, -3.140625, 3.140625), -3.140625, 3.140625)
    accepted = touch_ends(jax.random.randint(seeds[4], (4, NT, NX, NY, NZ), 0, NTRIAL), jax.random.fold_in(seeds[4], 1), 0, NTRIAL - 1).astype(jnp.int32)
    return {"links": links, "trials": trials, "cos_polar": cos_polar, "azimuth": azimuth, "accepted": accepted}


plaq_weight = 5.0 / 3.0
rect_weight = -1.0 / 12.0
coupling = 1.5

def quat_mul(left, right):
    return jnp.stack([left[0] * right[0] - left[1] * right[1] - left[2] * right[2] - left[3] * right[3], left[0] * right[1] + right[0] * left[1] - left[2] * right[3] + left[3] * right[2], left[0] * right[2] + right[0] * left[2] - left[3] * right[1] + left[1] * right[3], left[0] * right[3] + right[0] * left[3] - left[1] * right[2] + left[2] * right[1]])

def quat_conj(value):
    return jnp.concatenate([value[:1], -value[1:]], axis=0)

def chain_of(factors):
    return reduce(quat_mul, factors)

def staple_sum(lookup, along):
    plaq = 0.0
    rect = 0.0
    for across in range(4):
        if across == along:
            continue

        def link_at(direction, step_along, step_across):
            offset = tuple(((step_along if index == along else 0) + (step_across if index == across else 0) for index in range(4)))
            return lookup(direction, offset)

        def back_at(direction, step_along, step_across):
            return quat_conj(link_at(direction, step_along, step_across))
        plaq = plaq + chain_of([link_at(across, 1, 0), back_at(along, 0, 1), back_at(across, 0, 0)])
        plaq = plaq + chain_of([back_at(across, 1, -1), back_at(along, 0, -1), link_at(across, 0, -1)])
        rect = rect + chain_of([link_at(along, 1, 0), link_at(across, 2, 0), back_at(along, 1, 1), back_at(along, 0, 1), back_at(across, 0, 0)])
        rect = rect + chain_of([link_at(along, 1, 0), back_at(across, 2, -1), back_at(along, 1, -1), back_at(along, 0, -1), link_at(across, 0, -1)])
        rect = rect + chain_of([link_at(across, 1, 0), back_at(along, 0, 1), back_at(along, -1, 1), back_at(across, -1, 0), link_at(along, -1, 0)])
        rect = rect + chain_of([back_at(across, 1, -1), back_at(along, 0, -1), back_at(along, -1, -1), link_at(across, -1, -1), link_at(along, -1, 0)])
        rect = rect + chain_of([link_at(across, 1, 0), link_at(across, 1, 1), back_at(along, 0, 2), back_at(across, 0, 1), back_at(across, 0, 0)])
        rect = rect + chain_of([back_at(across, 1, -1), back_at(across, 1, -2), back_at(along, 0, -2), link_at(across, 0, -2), link_at(across, 0, -1)])
    return plaq_weight * plaq + rect_weight * rect

def pick_trials(trials, accepted):
    numbers = jnp.arange(trials.shape[0], dtype=jnp.int32).reshape(-1, 1, 1, 1, 1, 1)
    return lax.optimization_barrier(jnp.sum(jnp.where(accepted[None] == numbers, trials, jnp.float32(0.0)), axis=0))

def even_sites(t_start, x_start, y_start, shape):
    total = t_start + lax.broadcasted_iota(jnp.int32, shape, 0)
    total = total + x_start + lax.broadcasted_iota(jnp.int32, shape, 1)
    total = total + y_start + lax.broadcasted_iota(jnp.int32, shape, 2)
    total = total + lax.broadcasted_iota(jnp.int32, shape, 3)
    return total % 2 == 0

def heat_bath(old_link, staple, draw, cos_value, azimuth, even):
    size = jnp.sqrt(lax.optimization_barrier(jnp.sum(staple * staple, axis=0)))
    floor = jnp.maximum(size, 1.0)
    strength = coupling * floor
    low = jnp.exp(-2.0 * strength)
    head = 1.0 + jnp.log(low + (1.0 - low) * draw) / strength
    radius = jnp.sqrt(1.0 - head * head)
    side = jnp.sqrt(1.0 - cos_value * cos_value)
    trial = jnp.stack([head, radius * side * jnp.cos(azimuth), radius * side * jnp.sin(azimuth), radius * cos_value])
    updated = quat_mul(trial, quat_conj(staple)) / floor[None]
    return jnp.where(even[None], updated, old_link)

def reference(links, trials, cos_polar, azimuth, accepted):
    memo = {}

    def lookup(direction, offset):
        keyname = (direction, offset)
        if keyname not in memo:
            memo[keyname] = jnp.roll(links[direction], tuple((-value for value in offset)), axis=(1, 2, 3, 4))
        return memo[keyname]
    even = even_sites(jnp.int32(0), jnp.int32(0), jnp.int32(0), links.shape[2:])
    picked = pick_trials(trials, accepted)
    new_links = jnp.stack([heat_bath(links[direction], staple_sum(lookup, direction), picked[direction], cos_polar[direction], azimuth[direction], even) for direction in range(4)])
    transporters = lax.associative_scan(quat_mul, new_links[0], axis=1)
    return (new_links, transporters)
```

```python
import itertools

import jax
import jax.numpy as jnp
from jax import lax
from jax.experimental import pallas as pl
from jax.experimental.pallas import tpu as pltpu
from jax.sharding import PartitionSpec as P

plaq_weight = 5.0 / 3.0
rect_weight = -1.0 / 12.0
coupling = 1.5

MESH = pl.DeviceIdType.MESH
AXES = ("zt", "gx", "gy")
BITS = (4, 2, 1)


class Quat:
    def __init__(self, parts, flip=False):
        self.parts = tuple(parts)
        self.flip = flip

    def conj(self):
        return Quat(self.parts, not self.flip)

    def __mul__(self, other):
        if self.flip and other.flip:
            return (other.conj() * self.conj()).conj()
        a0, a1, a2, a3 = self.parts
        b0, b1, b2, b3 = other.parts
        if not self.flip and not other.flip:
            return Quat(
                (
                    (a0 * b0 - a1 * b1) - (a2 * b2 + a3 * b3),
                    (a0 * b1 + b0 * a1) - (a2 * b3 - a3 * b2),
                    (a0 * b2 + b0 * a2) - (a3 * b1 - a1 * b3),
                    (a0 * b3 + b0 * a3) - (a1 * b2 - a2 * b1),
                )
            )
        real = (a0 * b0 + a1 * b1) + (a2 * b2 + a3 * b3)
        if other.flip:
            return Quat(
                (
                    real,
                    (b0 * a1 - a0 * b1) + (a2 * b3 - a3 * b2),
                    (b0 * a2 - a0 * b2) + (a3 * b1 - a1 * b3),
                    (b0 * a3 - a0 * b3) + (a1 * b2 - a2 * b1),
                )
            )
        return Quat(
            (
                real,
                (a0 * b1 - b0 * a1) + (a2 * b3 - a3 * b2),
                (a0 * b2 - b0 * a2) + (a3 * b1 - a1 * b3),
                (a0 * b3 - b0 * a3) + (a1 * b2 - a2 * b1),
            )
        )

    def plain(self):
        if not self.flip:
            return self.parts
        return (self.parts[0],) + tuple(-part for part in self.parts[1:])

    def scaled(self, factor):
        return Quat(tuple(part * factor for part in self.parts), self.flip)

    def __add__(self, other):
        if self.flip == other.flip:
            return Quat(tuple(p + q for p, q in zip(self.parts, other.parts)), self.flip)
        (a0, a1, a2, a3), (b0, b1, b2, b3) = self.parts, other.parts
        return Quat((a0 + b0, a1 - b1, a2 - b2, a3 - b3), self.flip)


def canonical(offset, sizes):
    return tuple(1 if (step == -1 and size == 2) else step for step, size in zip(offset, sizes))


def halo_slots(sizes):
    slots = []
    for offset in itertools.product((0, 1, -1), repeat=3):
        used = [axis for axis in range(3) if offset[axis]]
        key = canonical(offset, sizes)
        if len(used) in (1, 2) and key not in slots:
            slots.append(key)
    return slots


def pieces_of(offset):
    used = [axis for axis in range(3) if offset[axis]]
    if len(used) == 1:
        return ((0, 4),)
    low, high = used
    if high == low + 1:
        return ((low, high + 1),)
    return ((low, low + 1), (high, high + 1))


def copies_of(sizes):
    slots = halo_slots(sizes)
    plan = [(slot, piece) for slot in slots for piece in pieces_of(slot)]

    def far(entry):
        offset = entry[0]
        return (-(2 * abs(offset[1]) + abs(offset[0])), entry)

    return slots, sorted(plan, key=far)


def kernel(sizes, links_hbm, trials_hbm, cos_hbm, azim_hbm, acc_hbm, new_hbm, trans_hbm,
           own, halo, trials, cosv, azim, acc, new, trans, total, gathered, before,
           local_sem, send_sem, recv_sem, tot_send, tot_recv):
    slots, plan = copies_of(sizes)
    me = tuple(lax.axis_index(name) for name in AXES)

    def device(offset):
        return {
            name: lax.rem(place + (step % size), size)
            for name, place, step, size in zip(AXES, me, offset, sizes)
        }

    laps = sizes[0]
    partners = list(slots)
    for lap in range(1, laps):
        key = (lap if lap < laps - 1 else -1, 0, 0)
        key = canonical(key, sizes)
        if key not in partners:
            partners.append(key)

    barrier = pltpu.get_barrier_semaphore()
    for offset in partners:
        pl.semaphore_signal(barrier, inc=1, device_id=device(offset), device_id_type=MESH)

    locals_ = [
        pltpu.make_async_copy(src, dst, local_sem.at[index])
        for index, (src, dst) in enumerate(
            ((links_hbm, own), (acc_hbm, acc), (trials_hbm, trials), (azim_hbm, azim), (cos_hbm, cosv))
        )
    ]
    for copy in locals_:
        copy.start()

    pl.semaphore_wait(barrier, len(partners))

    sends = {}
    for index, (slot, (first, stop)) in enumerate(plan):
        back = tuple(-step for step in slot)
        copy = pltpu.make_async_remote_copy(
            src_ref=links_hbm.at[pl.ds(first, stop - first)],
            dst_ref=halo.at[slots.index(slot), pl.ds(first, stop - first)],
            send_sem=send_sem.at[index],
            recv_sem=recv_sem.at[index],
            device_id=device(back),
            device_id_type=MESH,
        )
        copy.start()
        sends[(slot, first)] = copy

    rows, lanes = own.shape[2:]
    row = lax.broadcasted_iota(jnp.int32, (rows, lanes), 0)
    lane = lax.broadcasted_iota(jnp.int32, (rows, lanes), 1)
    bit = [(row // value) % 2 == 1 for value in BITS]
    even = (row // 4 + row // 2 + row + lane) % 2 == 0

    for copy in locals_:
        copy.wait()

    draws, polar, trig_cos, trig_sin = [], [], [], []
    for along in range(4):
        which = acc[along]
        draw = trials[0, along]
        for number in range(1, trials.shape[0]):
            draw = jnp.where(which == number, trials[number, along], draw)
        draws.append(draw)
        cosine = cosv[along]
        side = jnp.sqrt(1.0 - cosine * cosine)
        polar.append(cosine)
        trig_cos.append(side * jnp.cos(azim[along]))
        trig_sin.append(side * jnp.sin(azim[along]))

    arrived = set()

    def arrive(used):
        for slot, (first, stop) in plan:
            axes = {axis for axis in range(3) if slot[axis]}
            if axes <= used and (slot, first) not in arrived:
                arrived.add((slot, first))
                sends[(slot, first)].wait_recv()

    memo = {}

    def block(direction, part, blk):
        blk = canonical(blk, sizes)
        key = ("block", direction, part, blk)
        if key not in memo:
            if blk == (0, 0, 0):
                memo[key] = own[direction, part]
            else:
                memo[key] = halo[slots.index(blk), direction, part]
        return memo[key]

    def field(direction, part, blk, offset):
        blk = canonical(blk, sizes)
        key = (direction, part, blk, offset)
        if key in memo:
            return memo[key]
        if offset[3]:
            flat = field(direction, part, blk, offset[:3] + (0,))
            value = pltpu.roll(flat, (-offset[3]) % lanes, 1)
        else:
            moved = [axis for axis in range(3) if offset[axis]]
            if not moved:
                value = block(direction, part, blk)
            else:
                axis = moved[0]
                step = offset[axis]
                for other in moved:
                    if abs(offset[other]) == 2:
                        axis, step = other, offset[other]
                rest = offset[:axis] + (0,) + offset[axis + 1 :]
                sign = 1 if step > 0 else -1
                beyond = blk[:axis] + (sign,) + blk[axis + 1 :]
                far = field(direction, part, beyond, rest)
                if abs(step) == 2:
                    value = far
                else:
                    near = field(direction, part, blk, rest)
                    size = BITS[axis]
                    if size * 2 == rows:
                        mixed = jnp.where(bit[axis], near, far) if step > 0 else jnp.where(bit[axis], far, near)
                        value = pltpu.roll(mixed, size, 0)
                    elif step > 0:
                        value = jnp.where(bit[axis], pltpu.roll(far, size, 0), pltpu.roll(near, rows - size, 0))
                    else:
                        value = jnp.where(bit[axis], pltpu.roll(near, size, 0), pltpu.roll(far, rows - size, 0))
        memo[key] = value
        return value

    ending = [None] * 4
    leading = [None] * 4

    def add(store, along, value):
        value = Quat(value.plain())
        store[along] = value if store[along] is None else store[along] + value

    def pair(along, across):
        def at(direction, step_along, step_across):
            offset = [0, 0, 0, 0]
            offset[along] = step_along
            offset[across] = step_across
            return Quat(tuple(field(direction, part, (0, 0, 0), tuple(offset)) for part in range(4)))

        corner = at(across, 1, 0) * at(along, 0, 1).conj()
        wide = (at(along, 1, 0) * at(across, 2, 0)) * (at(along, 0, 1) * at(along, 1, 1)).conj()
        tall = (at(across, 1, 0) * at(across, 1, 1)) * (at(across, 0, 1) * at(along, 0, 2)).conj()
        add(ending, along, (corner.scaled(plaq_weight) + (wide + tall).scaled(rect_weight)) * at(across, 0, 0).conj())
        add(leading, along, corner * (at(across, -1, 0) * at(along, -1, 1)).conj())
        corner = (at(along, 0, -1) * at(across, 1, -1)).conj()
        wide = (at(along, 1, 0) * at(across, 2, -1).conj()) * (at(along, 0, -1) * at(along, 1, -1)).conj()
        tall = (at(across, 1, -2) * at(across, 1, -1)).conj() * (at(along, 0, -2).conj() * at(across, 0, -2))
        corner_plain = Quat(corner.plain())
        add(
            ending,
            along,
            (corner_plain.scaled(plaq_weight) + (wide + tall).scaled(rect_weight)) * at(across, 0, -1),
        )
        add(leading, along, corner * (at(along, -1, -1).conj() * at(across, -1, -1)))

    def heat_bath(along):
        offset = [0, 0, 0, 0]
        offset[along] = -1
        back = Quat(tuple(field(along, part, (0, 0, 0), tuple(offset)) for part in range(4)))
        staple = ending[along] + (leading[along] * back).scaled(rect_weight)
        s0, s1, s2, s3 = staple.parts
        size = jnp.sqrt((s0 * s0 + s1 * s1) + (s2 * s2 + s3 * s3))
        floor = jnp.maximum(size, 1.0)
        strength = coupling * floor
        low = jnp.exp(-2.0 * strength)
        head = 1.0 + jnp.log(low + (1.0 - low) * draws[along]) / strength
        radius = jnp.sqrt(1.0 - head * head)
        trial = Quat((head, radius * trig_cos[along], radius * trig_sin[along], radius * polar[along]))
        inverse = 1.0 / floor
        updated = (trial * staple.conj()).scaled(inverse)
        out = tuple(
            jnp.where(even, value, block(along, part, (0, 0, 0))) for part, value in enumerate(updated.parts)
        )
        for part in range(4):
            new[along, part] = out[part]
        return out

    arrive({2})
    pair(2, 3)
    pair(3, 2)
    arrive({0, 2})
    pair(0, 3)
    pair(0, 2)
    pair(3, 0)
    pair(2, 0)
    arrive({0, 1, 2})
    pair(0, 1)
    new_t = heat_bath(0)

    turned = tuple(pltpu.roll(part, 4, 0) for part in new_t)
    first = Quat(tuple(jnp.where(bit[0], b, a) for a, b in zip(new_t, turned)))
    second = Quat(tuple(jnp.where(bit[0], a, b) for a, b in zip(new_t, turned)))
    both = first * second
    inner = Quat(tuple(jnp.where(bit[0], b, a) for a, b in zip(first.parts, both.parts)))
    for part in range(4):
        total[part] = both.parts[part]

    def hop(lap):
        return pltpu.make_async_remote_copy(
            src_ref=total,
            dst_ref=gathered.at[lap],
            send_sem=tot_send.at[lap],
            recv_sem=tot_recv.at[lap],
            device_id=device((lap, 0, 0)),
            device_id_type=MESH,
        )

    for lap in range(laps - 1, 0, -1):

        @pl.when(me[0] + lap < laps)
        def _():
            hop(lap).start()

    for along, across in ((1, 0), (1, 2), (1, 3)):
        pair(along, across)
    heat_bath(1)
    pair(2, 1)
    heat_bath(2)
    pair(3, 1)
    heat_bath(3)
    out_new = pltpu.make_async_copy(new, new_hbm, local_sem.at[5])
    out_new.start()

    for part in range(4):
        before[part] = jnp.full((rows, lanes), 1.0 if part == 0 else 0.0, jnp.float32)
    for lap in range(laps - 1, 0, -1):

        @pl.when(me[0] >= lap)
        def _():
            hop(lap).wait_recv()
            state = Quat(tuple(before[part] for part in range(4)))
            state = state * Quat(tuple(gathered[lap, part] for part in range(4)))
            for part in range(4):
                before[part] = state.parts[part]

    final = Quat(tuple(before[part] for part in range(4))) * inner
    for part in range(4):
        trans[part] = final.parts[part]
    out_trans = pltpu.make_async_copy(trans, trans_hbm, local_sem.at[6])
    out_trans.start()

    for copy in sends.values():
        copy.wait_send()
    for lap in range(laps - 1, 0, -1):

        @pl.when(me[0] + lap < laps)
        def _():
            hop(lap).wait_send()

    out_new.wait()
    out_trans.wait()


def solution(mesh):
    sizes = tuple(mesh.shape[name] for name in AXES)

    def local(links, trials, cos_polar, azimuth, accepted):
        dirs, comps, t_len, x_len, y_len, z_len = links.shape
        assert (t_len, x_len, y_len) == (2, 2, 2)
        rows = t_len * x_len * y_len
        tile = (rows, z_len)
        slots, plan = copies_of(sizes)
        any_spec = pl.BlockSpec(memory_space=pl.ANY)
        f32 = jnp.float32

        def run(*args):
            return kernel(sizes, *args)

        new, trans = pl.pallas_call(
            run,
            out_shape=(
                jax.ShapeDtypeStruct((dirs, comps) + tile, f32),
                jax.ShapeDtypeStruct((comps,) + tile, f32),
            ),
            in_specs=[any_spec] * 5,
            out_specs=(any_spec, any_spec),
            scratch_shapes=[
                pltpu.VMEM((dirs, comps) + tile, f32),
                pltpu.VMEM((len(slots), dirs, comps) + tile, f32),
                pltpu.VMEM((trials.shape[0], dirs) + tile, f32),
                pltpu.VMEM((dirs,) + tile, f32),
                pltpu.VMEM((dirs,) + tile, f32),
                pltpu.VMEM((dirs,) + tile, jnp.int32),
                pltpu.VMEM((dirs, comps) + tile, f32),
                pltpu.VMEM((comps,) + tile, f32),
                pltpu.VMEM((comps,) + tile, f32),
                pltpu.VMEM((sizes[0], comps) + tile, f32),
                pltpu.VMEM((comps,) + tile, f32),
                pltpu.SemaphoreType.DMA((7,)),
                pltpu.SemaphoreType.DMA((len(plan),)),
                pltpu.SemaphoreType.DMA((len(plan),)),
                pltpu.SemaphoreType.DMA((sizes[0],)),
                pltpu.SemaphoreType.DMA((sizes[0],)),
            ],
            compiler_params=pltpu.CompilerParams(collective_id=0, has_side_effects=True),
        )(
            links.reshape((dirs, comps) + tile),
            trials.reshape((trials.shape[0], dirs) + tile),
            cos_polar.reshape((dirs,) + tile),
            azimuth.reshape((dirs,) + tile),
            accepted.reshape((dirs,) + tile),
        )
        return new.reshape(links.shape), trans.reshape(links.shape[1:])

    return jax.shard_map(
        local,
        mesh=mesh,
        in_specs=(
            P(None, None, "zt", "gx", "gy", None),
            P(None, None, "zt", "gx", "gy", None),
            P(None, "zt", "gx", "gy", None),
            P(None, "zt", "gx", "gy", None),
            P(None, "zt", "gx", "gy", None),
        ),
        out_specs=(P(None, None, "zt", "gx", "gy", None), P(None, "zt", "gx", "gy", None)),
        check_vma=False,
    )
```

```python
import itertools

import jax
import jax.numpy as jnp
from jax import lax
from jax.experimental import pallas as pl
from jax.experimental.pallas import tpu as pltpu
from jax.sharding import PartitionSpec as P

plaq_weight = 5.0 / 3.0
rect_weight = -1.0 / 12.0
coupling = 1.5

MESH = pl.DeviceIdType.MESH
AXES = ("zt", "gx", "gy")
BITS = (4, 2, 1)


class Quat:
    def __init__(self, parts, flip=False):
        self.parts = tuple(parts)
        self.flip = flip

    def conj(self):
        return Quat(self.parts, not self.flip)

    def __mul__(self, other):
        if self.flip and other.flip:
            return (other.conj() * self.conj()).conj()
        a0, a1, a2, a3 = self.parts
        b0, b1, b2, b3 = other.parts
        if not self.flip and not other.flip:
            return Quat(
                (
                    (a0 * b0 - a1 * b1) - (a2 * b2 + a3 * b3),
                    (a0 * b1 + b0 * a1) - (a2 * b3 - a3 * b2),
                    (a0 * b2 + b0 * a2) - (a3 * b1 - a1 * b3),
                    (a0 * b3 + b0 * a3) - (a1 * b2 - a2 * b1),
                )
            )
        real = (a0 * b0 + a1 * b1) + (a2 * b2 + a3 * b3)
        if other.flip:
            return Quat(
                (
                    real,
                    (b0 * a1 - a0 * b1) + (a2 * b3 - a3 * b2),
                    (b0 * a2 - a0 * b2) + (a3 * b1 - a1 * b3),
                    (b0 * a3 - a0 * b3) + (a1 * b2 - a2 * b1),
                )
            )
        return Quat(
            (
                real,
                (a0 * b1 - b0 * a1) + (a2 * b3 - a3 * b2),
                (a0 * b2 - b0 * a2) + (a3 * b1 - a1 * b3),
                (a0 * b3 - b0 * a3) + (a1 * b2 - a2 * b1),
            )
        )

    def plain(self):
        if not self.flip:
            return self.parts
        return (self.parts[0],) + tuple(-part for part in self.parts[1:])

    def scaled(self, factor):
        return Quat(tuple(part * factor for part in self.parts), self.flip)

    def __add__(self, other):
        if self.flip == other.flip:
            return Quat(tuple(p + q for p, q in zip(self.parts, other.parts)), self.flip)
        (a0, a1, a2, a3), (b0, b1, b2, b3) = self.parts, other.parts
        return Quat((a0 + b0, a1 - b1, a2 - b2, a3 - b3), self.flip)


def canonical(offset, sizes):
    return tuple(1 if (step == -1 and size == 2) else step for step, size in zip(offset, sizes))


def halo_slots(sizes):
    slots = []
    for offset in itertools.product((0, 1, -1), repeat=3):
        used = [axis for axis in range(3) if offset[axis]]
        key = canonical(offset, sizes)
        if len(used) in (1, 2) and key not in slots:
            slots.append(key)
    return slots


def pieces_of(offset, sizes):
    used = [axis for axis in range(3) if offset[axis]]
    if len(used) == 1:
        return (((0, 4), (0, 8)),)
    low, high = used
    both = sizes[high] == 2
    ends = {low: 0 if offset[low] > 0 else 1}
    if not both:
        ends[high] = 0 if offset[high] > 0 else 1
    rows = [
        row for row in range(8) if all((row // BITS[axis]) % 2 == end for axis, end in ends.items())
    ]
    runs = []
    for row in rows:
        if runs and runs[-1][0] + runs[-1][1] == row:
            runs[-1][1] += 1
        else:
            runs.append([row, 1])
    whole = set()
    if offset[low] > 0 and (both or offset[high] < 0):
        whole.add(high)
    if offset[low] < 0 and (both or offset[high] > 0):
        whole.add(low)
    if not whole and high == low + 1:
        return tuple(((low, 2), tuple(run)) for run in runs)
    pieces = []
    for axis in used:
        for run in [(0, 8)] if axis in whole else runs:
            pieces.append(((axis, 1), tuple(run)))
    return tuple(pieces)


def copies_of(sizes):
    slots = halo_slots(sizes)
    plan = [(slot, piece) for slot in slots for piece in pieces_of(slot, sizes)]

    def far(entry):
        offset = entry[0]
        return (-(2 * abs(offset[1]) + abs(offset[0])), entry)

    return slots, sorted(plan, key=far)


def kernel(sizes, links_hbm, trials_hbm, cos_hbm, azim_hbm, acc_hbm, new, trans,
           own, halo, trials, cosv, azim, acc, total, gathered, before,
           local_sem, send_sem, recv_sem, tot_send, tot_recv):
    slots, plan = copies_of(sizes)
    me = tuple(lax.axis_index(name) for name in AXES)

    def device(offset):
        return {
            name: lax.rem(place + (step % size), size)
            for name, place, step, size in zip(AXES, me, offset, sizes)
        }

    laps = sizes[0]
    partners = list(slots)
    for lap in range(1, laps):
        key = (lap if lap < laps - 1 else -1, 0, 0)
        key = canonical(key, sizes)
        if key not in partners:
            partners.append(key)

    barrier = pltpu.get_barrier_semaphore()
    for offset in partners:
        pl.semaphore_signal(barrier, inc=1, device_id=device(offset), device_id_type=MESH)

    locals_ = [
        pltpu.make_async_copy(src, dst, local_sem.at[index])
        for index, (src, dst) in enumerate(
            ((links_hbm, own), (acc_hbm, acc), (trials_hbm, trials), (azim_hbm, azim), (cos_hbm, cosv))
        )
    ]
    for copy in locals_:
        copy.start()

    pl.semaphore_wait(barrier, len(partners))

    sends = {}
    for index, (slot, piece) in enumerate(plan):
        (first, count), (start, length) = piece
        back = tuple(-step for step in slot)
        copy = pltpu.make_async_remote_copy(
            src_ref=links_hbm.at[pl.ds(first, count), :, pl.ds(start, length)],
            dst_ref=halo.at[slots.index(slot), pl.ds(first, count), :, pl.ds(start, length)],
            send_sem=send_sem.at[index],
            recv_sem=recv_sem.at[index],
            device_id=device(back),
            device_id_type=MESH,
        )
        copy.start()
        sends[(slot, piece)] = copy

    rows, lanes = own.shape[2:]
    row = lax.broadcasted_iota(jnp.int32, (rows, lanes), 0)
    lane = lax.broadcasted_iota(jnp.int32, (rows, lanes), 1)
    bit = [(row // value) % 2 == 1 for value in BITS]
    even = (row // 4 + row // 2 + row + lane) % 2 == 0

    for copy in locals_:
        copy.wait()

    draws, polar, trig_cos, trig_sin = [], [], [], []
    for along in range(4):
        which = acc[along]
        draw = trials[0, along]
        for number in range(1, trials.shape[0]):
            draw = jnp.where(which == number, trials[number, along], draw)
        draws.append(draw)
        cosine = cosv[along]
        side = jnp.sqrt(1.0 - cosine * cosine)
        polar.append(cosine)
        trig_cos.append(side * jnp.cos(azim[along]))
        trig_sin.append(side * jnp.sin(azim[along]))

    arrived = set()

    def arrive(used):
        for slot, piece in plan:
            axes = {axis for axis in range(3) if slot[axis]}
            if axes <= used and (slot, piece) not in arrived:
                arrived.add((slot, piece))
                sends[(slot, piece)].wait_recv()

    memo = {}

    def block(direction, part, blk):
        blk = canonical(blk, sizes)
        key = ("block", direction, part, blk)
        if key not in memo:
            if blk == (0, 0, 0):
                memo[key] = own[direction, part]
            else:
                memo[key] = halo[slots.index(blk), direction, part]
        return memo[key]

    def field(direction, part, blk, offset):
        blk = canonical(blk, sizes)
        key = (direction, part, blk, offset)
        if key in memo:
            return memo[key]
        if offset[3]:
            flat = field(direction, part, blk, offset[:3] + (0,))
            value = pltpu.roll(flat, (-offset[3]) % lanes, 1)
        else:
            moved = [axis for axis in range(3) if offset[axis]]
            if not moved:
                value = block(direction, part, blk)
            else:
                axis = moved[0]
                step = offset[axis]
                for other in moved:
                    if abs(offset[other]) == 2:
                        axis, step = other, offset[other]
                rest = offset[:axis] + (0,) + offset[axis + 1 :]
                sign = 1 if step > 0 else -1
                beyond = blk[:axis] + (sign,) + blk[axis + 1 :]
                far = field(direction, part, beyond, rest)
                if abs(step) == 2:
                    value = far
                else:
                    near = field(direction, part, blk, rest)
                    size = BITS[axis]
                    if size * 2 == rows:
                        mixed = jnp.where(bit[axis], near, far) if step > 0 else jnp.where(bit[axis], far, near)
                        value = pltpu.roll(mixed, size, 0)
                    elif step > 0:
                        value = jnp.where(bit[axis], pltpu.roll(far, size, 0), pltpu.roll(near, rows - size, 0))
                    else:
                        value = jnp.where(bit[axis], pltpu.roll(near, size, 0), pltpu.roll(far, rows - size, 0))
        memo[key] = value
        return value

    ending = [None] * 4
    leading = [None] * 4

    def add(store, along, value):
        value = Quat(value.plain())
        store[along] = value if store[along] is None else store[along] + value

    def pair(along, across):
        def at(direction, step_along, step_across):
            offset = [0, 0, 0, 0]
            offset[along] = step_along
            offset[across] = step_across
            return Quat(tuple(field(direction, part, (0, 0, 0), tuple(offset)) for part in range(4)))

        corner = at(across, 1, 0) * at(along, 0, 1).conj()
        wide = (at(along, 1, 0) * at(across, 2, 0)) * (at(along, 0, 1) * at(along, 1, 1)).conj()
        tall = (at(across, 1, 0) * at(across, 1, 1)) * (at(across, 0, 1) * at(along, 0, 2)).conj()
        add(ending, along, (corner.scaled(plaq_weight) + (wide + tall).scaled(rect_weight)) * at(across, 0, 0).conj())
        add(leading, along, corner * (at(across, -1, 0) * at(along, -1, 1)).conj())
        corner = (at(along, 0, -1) * at(across, 1, -1)).conj()
        wide = (at(along, 1, 0) * at(across, 2, -1).conj()) * (at(along, 0, -1) * at(along, 1, -1)).conj()
        tall = (at(across, 1, -2) * at(across, 1, -1)).conj() * (at(along, 0, -2).conj() * at(across, 0, -2))
        corner_plain = Quat(corner.plain())
        add(
            ending,
            along,
            (corner_plain.scaled(plaq_weight) + (wide + tall).scaled(rect_weight)) * at(across, 0, -1),
        )
        add(leading, along, corner * (at(along, -1, -1).conj() * at(across, -1, -1)))

    def heat_bath(along):
        offset = [0, 0, 0, 0]
        offset[along] = -1
        back = Quat(tuple(field(along, part, (0, 0, 0), tuple(offset)) for part in range(4)))
        staple = ending[along] + (leading[along] * back).scaled(rect_weight)
        s0, s1, s2, s3 = staple.parts
        size = jnp.sqrt((s0 * s0 + s1 * s1) + (s2 * s2 + s3 * s3))
        floor = jnp.maximum(size, 1.0)
        strength = coupling * floor
        low = jnp.exp(-2.0 * strength)
        head = 1.0 + jnp.log(low + (1.0 - low) * draws[along]) / strength
        radius = jnp.sqrt(1.0 - head * head)
        trial = Quat((head, radius * trig_cos[along], radius * trig_sin[along], radius * polar[along]))
        inverse = 1.0 / floor
        updated = (trial * staple.conj()).scaled(inverse)
        out = tuple(
            jnp.where(even, value, block(along, part, (0, 0, 0))) for part, value in enumerate(updated.parts)
        )
        for part in range(4):
            new[along, part] = out[part]
        return out

    arrive({2})
    pair(2, 3)
    pair(3, 2)
    arrive({0, 2})
    pair(0, 3)
    pair(0, 2)
    pair(3, 0)
    pair(2, 0)
    arrive({0, 1, 2})
    pair(0, 1)
    new_t = heat_bath(0)

    turned = tuple(pltpu.roll(part, 4, 0) for part in new_t)
    first = Quat(tuple(jnp.where(bit[0], b, a) for a, b in zip(new_t, turned)))
    second = Quat(tuple(jnp.where(bit[0], a, b) for a, b in zip(new_t, turned)))
    both = first * second
    inner = Quat(tuple(jnp.where(bit[0], b, a) for a, b in zip(first.parts, both.parts)))
    for part in range(4):
        total[part] = both.parts[part]

    def hop(lap):
        return pltpu.make_async_remote_copy(
            src_ref=total,
            dst_ref=gathered.at[lap],
            send_sem=tot_send.at[lap],
            recv_sem=tot_recv.at[lap],
            device_id=device((lap, 0, 0)),
            device_id_type=MESH,
        )

    for lap in range(laps - 1, 0, -1):

        @pl.when(me[0] + lap < laps)
        def _():
            hop(lap).start()

    for along, across in ((1, 0), (1, 2), (1, 3)):
        pair(along, across)
    heat_bath(1)
    pair(2, 1)
    heat_bath(2)
    pair(3, 1)
    heat_bath(3)

    for part in range(4):
        before[part] = jnp.full((rows, lanes), 1.0 if part == 0 else 0.0, jnp.float32)
    for lap in range(laps - 1, 0, -1):

        @pl.when(me[0] >= lap)
        def _():
            hop(lap).wait_recv()
            state = Quat(tuple(before[part] for part in range(4)))
            state = state * Quat(tuple(gathered[lap, part] for part in range(4)))
            for part in range(4):
                before[part] = state.parts[part]

    final = Quat(tuple(before[part] for part in range(4))) * inner
    for part in range(4):
        trans[part] = final.parts[part]

    for copy in sends.values():
        copy.wait_send()
    for lap in range(laps - 1, 0, -1):

        @pl.when(me[0] + lap < laps)
        def _():
            hop(lap).wait_send()


def solution(mesh):
    sizes = tuple(mesh.shape[name] for name in AXES)

    def local(links, trials, cos_polar, azimuth, accepted):
        dirs, comps, t_len, x_len, y_len, z_len = links.shape
        assert (t_len, x_len, y_len) == (2, 2, 2)
        rows = t_len * x_len * y_len
        tile = (rows, z_len)
        slots, plan = copies_of(sizes)
        any_spec = pl.BlockSpec(memory_space=pl.ANY)
        f32 = jnp.float32

        def run(*args):
            return kernel(sizes, *args)

        new, trans = pl.pallas_call(
            run,
            out_shape=(
                pltpu.VMEM((dirs, comps) + tile, f32),
                pltpu.VMEM((comps,) + tile, f32),
            ),
            in_specs=[any_spec] * 5,
            out_specs=(pl.BlockSpec(memory_space=pltpu.VMEM),) * 2,
            scratch_shapes=[
                pltpu.VMEM((dirs, comps) + tile, f32),
                pltpu.VMEM((len(slots), dirs, comps) + tile, f32),
                pltpu.VMEM((trials.shape[0], dirs) + tile, f32),
                pltpu.VMEM((dirs,) + tile, f32),
                pltpu.VMEM((dirs,) + tile, f32),
                pltpu.VMEM((dirs,) + tile, jnp.int32),
                pltpu.VMEM((comps,) + tile, f32),
                pltpu.VMEM((sizes[0], comps) + tile, f32),
                pltpu.VMEM((comps,) + tile, f32),
                pltpu.SemaphoreType.DMA((5,)),
                pltpu.SemaphoreType.DMA((len(plan),)),
                pltpu.SemaphoreType.DMA((len(plan),)),
                pltpu.SemaphoreType.DMA((sizes[0],)),
                pltpu.SemaphoreType.DMA((sizes[0],)),
            ],
            compiler_params=pltpu.CompilerParams(collective_id=0, has_side_effects=True),
        )(
            links.reshape((dirs, comps) + tile),
            trials.reshape((trials.shape[0], dirs) + tile),
            cos_polar.reshape((dirs,) + tile),
            azimuth.reshape((dirs,) + tile),
            accepted.reshape((dirs,) + tile),
        )
        return new.reshape(links.shape), trans.reshape(links.shape[1:])

    return jax.shard_map(
        local,
        mesh=mesh,
        in_specs=(
            P(None, None, "zt", "gx", "gy", None),
            P(None, None, "zt", "gx", "gy", None),
            P(None, "zt", "gx", "gy", None),
            P(None, "zt", "gx", "gy", None),
            P(None, "zt", "gx", "gy", None),
        ),
        out_specs=(P(None, None, "zt", "gx", "gy", None), P(None, "zt", "gx", "gy", None)),
        check_vma=False,
    )
```
